32 devices in a mesh: dp: 8 (over y, x, core), tensor: 4 (over z).
Axes of the slice: x: 2, y: 2, z: 4, core: 2. Of those that a mesh axis runs over, the one named last changes fastest.
Arguments:
- tokens: bfloat16 [4096, 1024], P(('dp', 'tensor')), may hold values from -8 to 8
- qkv_weight: bfloat16 [3, 1024, 1024], P(None, 'dp', 'tensor'), may hold values from -1.0625 to 1.0625
- qkv_bias: float32 [3, 1024], P(None, 'tensor'), may hold values from -4 to 4
- out_weight: bfloat16 [1024, 1024], P('dp', 'tensor'), may hold values from -0.75 to 0.75
- out_bias: float32 [1024], replicated, may hold values from -6 to 6
- up_weight: bfloat16 [1024, 4096], P('dp', 'tensor'), may hold values from -0.1875 to 0.1875
- up_bias: float32 [4096], P('tensor'), may hold values from -6 to 6
- down_weight: bfloat16 [1024, 4096], P('dp', 'tensor'), may hold values from -0.09375 to 0.09375
- down_bias: float32 [1024], replicated, may hold values from -6 to 6
- gain_first: float32 [1024], replicated, may hold values from 0.5 to 1.5
- shift_first: float32 [1024], replicated, may hold values from -4 to 4
- gain_second: float32 [1024], replicated, may hold values from 0.5 to 1.5
- shift_second: float32 [1024], replicated, may hold values from -4 to 4
- cotangent: bfloat16 [4096, 1024], P(('dp', 'tensor')), may hold values from -6 to 6
Outputs:
- outputs: bfloat16 [4096, 1024], P(('dp', 'tensor'))
- grad_tokens: float32 [4096, 1024], P(('dp', 'tensor'))
- grad_qkv: float32 [3, 1024, 1024], P(None, 'dp', 'tensor')
- grad_qkvbias: float32 [3, 1024], P(None, 'tensor')
- grad_out: float32 [1024, 1024], P('dp', 'tensor')
- grad_outbias: float32 [1024], replicated
- grad_up: float32 [1024, 4096], P('dp', 'tensor')
- grad_upbias: float32 [4096], P('tensor')
- grad_down: float32 [1024, 4096], P('dp', 'tensor')
- grad_downbias: float32 [1024], replicated
- grad_gainfirst: float32 [1024], replicated
- grad_shiftfirst: float32 [1024], replicated
- grad_gainsecond: float32 [1024], replicated
- grad_shiftsecond: float32 [1024], replicated
The draws below stay inside these ranges and needn't reach their ends.
All inputs are finite; a program needn't handle non-finite values.
Results may differ from the reference program's by a relative error of at most 0.029.
The reference program's roundings to bfloat16 on the way count: a program that leaves them out, or rounds other values in their place, can miss the bound.
Values may be sent and summed in bfloat16 or wider, within the bound.
A program may use at most 128 MiB of HBM per device.

```python
import math
import jax
import jax.numpy as jnp
from jax import lax

D = 1024
HD = 64
ROT = 16
FF = 4096
SEQ = 512
TOKENS = 4096


def draw_tokens(key, part):
    first = jax.random.fold_in(key, 0)
    base = jnp.clip(jax.random.normal(first, (TOKENS, D), jnp.float32), -6.0, 6.0)
    return base.astype(jnp.bfloat16)


def draw_qkv_weight(key, part):
    first = jax.random.fold_in(key, 0)
    base = jnp.clip(jax.random.normal(first, (3, D, D), jnp.float32), -4.0, 4.0) * D ** (-0.5)
    return base.astype(jnp.bfloat16)


def spiked(drawn, rng, source, target, shards_of, factor):
    def block_of(dim):
        return (jnp.arange(drawn.shape[dim]) // (drawn.shape[dim] // shards_of)).reshape((-1,) + (1,) * (drawn.ndim - 1 - dim))

    first = jax.random.permutation(rng, shards_of)[block_of(target)]
    second = (block_of(target) + shards_of // 2) % shards_of
    return jnp.where((block_of(source) == first) | (block_of(source) == second), factor * drawn, drawn)


def block_scale(rng, extent, cuts, low, largest):
    factor_of = 1.0
    for axis_at, shards_of in cuts:
        steps = jax.random.uniform(jax.random.fold_in(jax.random.fold_in(rng, 6), axis_at), (shards_of,), jnp.float32, low / len(cuts), largest / len(cuts))
        factor_of = factor_of * jnp.repeat(jnp.exp(steps), extent[axis_at] // shards_of).reshape((-1,) + (1,) * (len(extent) - 1 - axis_at))
    return factor_of


def normal_values(rng, shape, spread, bound, shards=(), dtype=jnp.bfloat16):
    level = block_scale(rng, shape, shards, -0.22, 0.18) if shards else 1.0
    array = jax.random.normal(rng, shape, jnp.float32) * spread * level
    return jnp.minimum(jnp.maximum(array, -bound), bound).astype(dtype)


def gaussian_with(rng, dims, scale, limit, cuts, heavy, dtype=jnp.bfloat16):
    values = scale * jax.random.normal(rng, dims, jnp.float32)
    if cuts:
        values = values * block_scale(rng, dims, cuts, -0.22, 0.18)
    return jnp.clip(spiked(values, jax.random.fold_in(rng, 3), *heavy), -limit, limit).astype(dtype)


def setup_inputs(seed: int = 0) -> dict:
    key_list = jax.random.split(jax.random.key(seed), 15)
    return {
        "tokens": draw_tokens(jax.random.fold_in(key_list[14], 71), 0),
        "qkv_weight": draw_qkv_weight(jax.random.fold_in(key_list[14], 71), 0),
        "qkv_bias": normal_values(key_list[2], (3, D), 0.3, 4.0, ((1, 4),), jnp.float32),
        "out_weight": normal_values(key_list[3], (D, D), (D // 16) ** -0.5, 0.75, ((0, 8), (1, 4))),
        "out_bias": normal_values(key_list[4], (D,), 0.5, 6.0, (), jnp.float32),
        "up_weight": normal_values(key_list[5], (D, FF), D ** -0.5, 0.1875, ((0, 8), (1, 4))),
        "up_bias": normal_values(key_list[6], (FF,), 0.5, 6.0, ((0, 4),), jnp.float32),
        "down_weight": normal_values(key_list[7], (D, FF), FF ** -0.5, 0.09375, ((0, 8), (1, 4))),
        "down_bias": normal_values(key_list[8], (D,), 0.5, 6.0, (), jnp.float32),
        "gain_first": jnp.clip(1.0 + 0.1 * jax.random.normal(key_list[9], (D,), jnp.float32), 0.5, 1.5),
        "shift_first": normal_values(key_list[10], (D,), 0.3, 4.0, (), jnp.float32),
        "gain_second": jnp.clip(1.0 + 0.1 * jax.random.normal(key_list[11], (D,), jnp.float32), 0.5, 1.5),
        "shift_second": normal_values(key_list[12], (D,), 0.3, 4.0, (), jnp.float32),
        "cotangent": gaussian_with(key_list[13], (TOKENS, D), 1.0, 6.0, ((0, 32),), (0, 1, 32, 2.75)),
    }


epsilon = 1e-05

def rounded(values):
    return lax.optimization_barrier(values.astype(jnp.bfloat16)).astype(jnp.float32)

def normalize(rows):
    mean = lax.optimization_barrier(jnp.mean(rows, axis=-1, keepdims=True))
    centred = rows - mean
    variance = lax.optimization_barrier(jnp.mean(centred * centred, axis=-1, keepdims=True))
    inverse = lax.rsqrt(variance + epsilon)
    return (centred * inverse, inverse)

def gelu_exact(values):
    return jax.nn.gelu(values, approximate=False)

def tables(length, rot):
    half = rot // 2
    positions = jnp.arange(length).astype(jnp.float32)
    freqs = 10000.0 ** (-2.0 * jnp.arange(half).astype(jnp.float32) / rot)
    angles = positions[:, None] * freqs[None, :]
    cosine = jnp.concatenate([jnp.cos(angles), jnp.cos(angles)], -1)[:, None, :]
    sine = jnp.concatenate([jnp.sin(angles), jnp.sin(angles)], -1)[:, None, :]
    return (cosine, sine)

def rotate(values, cosine, sine):
    rot = cosine.shape[-1]
    half = rot // 2
    part = values[..., :rot]
    turned = jnp.concatenate([-part[..., half:], part[..., :half]], -1)
    return jnp.concatenate([part * cosine + turned * sine, values[..., rot:]], -1)

def rotate_back(grads, cosine, sine):
    rot = cosine.shape[-1]
    half = rot // 2
    part = grads[..., :rot]
    scaled = part * sine
    back = jnp.concatenate([scaled[..., half:], -scaled[..., :half]], -1)
    return jnp.concatenate([part * cosine + back, grads[..., rot:]], -1)

def masked(scores, index, block, length):
    rows = index * block + jnp.arange(block).astype(jnp.int32)
    cols = jnp.arange(length).astype(jnp.int32)
    return jnp.where((rows[:, None] >= cols[None, :])[None], scores, -1e+30)

def attend(query, keys, values):
    length, heads, width = query.shape
    block = min(length, 512)
    count = length // block
    scale = 1.0 / math.sqrt(width)
    keyf = keys.astype(jnp.float32)
    valuef = values.astype(jnp.float32)
    blocks = query.reshape(count, block, heads, width)

    def step(carry, item):
        qblock, index = item
        scores = jnp.einsum('qhd,khd->hqk', qblock.astype(jnp.float32), keyf) * scale
        scores = masked(scores, index, block, length)
        top = lax.optimization_barrier(jnp.max(scores, -1, keepdims=True))
        total = lax.optimization_barrier(jnp.sum(jnp.exp(scores - top), -1, keepdims=True))
        lse = top + jnp.log(total)
        probs = rounded(jnp.exp(scores - lse))
        context = jnp.einsum('hqk,khd->qhd', probs, valuef)
        return (carry, (context.astype(jnp.bfloat16), lse[..., 0]))
    indices = jnp.arange(count).astype(jnp.int32)
    _, (context, lse) = lax.scan(step, jnp.zeros((), jnp.float32), (blocks, indices))
    return (context.reshape(length, heads, width), lse)

def attend_back(query, keys, values, lse, dcontext):
    length, heads, width = query.shape
    block = min(length, 512)
    count = length // block
    scale = 1.0 / math.sqrt(width)
    keyf = keys.astype(jnp.float32)
    valuef = values.astype(jnp.float32)
    qblocks = query.reshape(count, block, heads, width)
    gblocks = dcontext.reshape(count, block, heads, width)

    def step(carry, item):
        dkeys, dvalues = carry
        qblock, lblock, gblock, index = item
        qfloat = qblock.astype(jnp.float32)
        gfloat = gblock.astype(jnp.float32)
        scores = jnp.einsum('qhd,khd->hqk', qfloat, keyf) * scale
        scores = masked(scores, index, block, length)
        weights = jnp.exp(scores - lblock[..., None])
        dvalues = dvalues + jnp.einsum('hqk,qhd->khd', rounded(weights), gfloat)
        dprobs = jnp.einsum('qhd,khd->hqk', gfloat, valuef)
        delta = lax.optimization_barrier(jnp.sum(weights * dprobs, -1, keepdims=True))
        dscores = rounded(weights * (dprobs - delta) * scale)
        dquery = jnp.einsum('hqk,khd->qhd', dscores, keyf)
        dkeys = dkeys + jnp.einsum('hqk,qhd->khd', dscores, qfloat)
        return ((dkeys, dvalues), dquery)
    start = (jnp.zeros(keys.shape, jnp.float32), jnp.zeros(keys.shape, jnp.float32))
    indices = jnp.arange(count).astype(jnp.int32)
    (dkeys, dvalues), dquery = lax.scan(step, start, (qblocks, lse, gblocks, indices))
    return (dquery.reshape(length, heads, width), dkeys, dvalues)

def sequence(rows, cot, qkv_weight, qkv_bias, out_weight, out_bias, up_weight, up_bias, down_weight, down_bias, gain_first, shift_first, gain_second, shift_second):
    length, width = rows.shape
    heads = width // HD
    rowsf = rows.astype(jnp.float32)
    normal, inverse = normalize(rowsf)
    first = (normal * gain_first + shift_first).astype(jnp.bfloat16)
    second = (normal * gain_second + shift_second).astype(jnp.bfloat16)
    projected = jnp.stack([jnp.dot(first, qkv_weight[j], preferred_element_type=jnp.float32) for j in range(3)])
    projected = projected + qkv_bias[:, None, :]
    cosine, sine = tables(length, ROT)
    query = rotate(projected[0].reshape(length, heads, HD), cosine, sine).astype(jnp.bfloat16)
    keys = rotate(projected[1].reshape(length, heads, HD), cosine, sine).astype(jnp.bfloat16)
    values = projected[2].reshape(length, heads, HD).astype(jnp.bfloat16)
    context, lse = attend(query, keys, values)
    context = context.reshape(length, width)
    pre = jnp.dot(second, up_weight, preferred_element_type=jnp.float32) + up_bias
    hidden = gelu_exact(pre).astype(jnp.bfloat16)
    branch = jnp.dot(context, out_weight.T, preferred_element_type=jnp.float32)
    branch = branch + jnp.dot(hidden, down_weight.T, preferred_element_type=jnp.float32)
    outputs = (rowsf + branch + out_bias + down_bias).astype(jnp.bfloat16)
    cotf = cot.astype(jnp.float32)
    bias_grad = lax.optimization_barrier(jnp.sum(cotf, 0))
    grad_out = jnp.dot(cot.T, context, preferred_element_type=jnp.float32)
    grad_down = jnp.dot(cot.T, hidden, preferred_element_type=jnp.float32)
    dcontext = jnp.dot(cot, out_weight, preferred_element_type=jnp.float32).astype(jnp.bfloat16)
    dhidden = jnp.dot(cot, down_weight, preferred_element_type=jnp.float32)
    _, pullback = jax.vjp(gelu_exact, pre)
    dpre = pullback(dhidden)[0]
    grad_upbias = lax.optimization_barrier(jnp.sum(dpre, 0))
    dpre16 = dpre.astype(jnp.bfloat16)
    grad_up = jnp.dot(second.T, dpre16, preferred_element_type=jnp.float32)
    dsecond = jnp.dot(dpre16, up_weight.T, preferred_element_type=jnp.float32)
    dquery, dkeys, dvalues = attend_back(query, keys, values, lse, dcontext.reshape(length, heads, HD))
    dquery = rotate_back(dquery, cosine, sine).reshape(length, width)
    dkeys = rotate_back(dkeys, cosine, sine).reshape(length, width)
    dprojected = jnp.stack([dquery, dkeys, dvalues.reshape(length, width)])
    grad_qkvbias = lax.optimization_barrier(jnp.sum(dprojected, 1))
    dprojected16 = dprojected.astype(jnp.bfloat16)
    grad_qkv = jnp.stack([jnp.dot(first.T, dprojected16[j], preferred_element_type=jnp.float32) for j in range(3)])
    dfirst = jnp.dot(dprojected16[0], qkv_weight[0].T, preferred_element_type=jnp.float32)
    dfirst = dfirst + jnp.dot(dprojected16[1], qkv_weight[1].T, preferred_element_type=jnp.float32)
    dfirst = dfirst + jnp.dot(dprojected16[2], qkv_weight[2].T, preferred_element_type=jnp.float32)
    grad_gainfirst = lax.optimization_barrier(jnp.sum(dfirst * normal, 0))
    grad_shiftfirst = lax.optimization_barrier(jnp.sum(dfirst, 0))
    grad_gainsecond = lax.optimization_barrier(jnp.sum(dsecond * normal, 0))
    grad_shiftsecond = lax.optimization_barrier(jnp.sum(dsecond, 0))
    mixed = gain_first * dfirst + gain_second * dsecond
    centred = mixed - lax.optimization_barrier(jnp.mean(mixed, -1, keepdims=True)) - normal * lax.optimization_barrier(jnp.mean(mixed * normal, -1, keepdims=True))
    grad_tokens = cotf + inverse * centred
    grads = (grad_qkv, grad_qkvbias, grad_out, bias_grad, grad_up, grad_upbias, grad_down, grad_gainfirst, grad_shiftfirst, grad_gainsecond, grad_shiftsecond)
    return (outputs, grad_tokens, grads)

def reference(tokens, qkv_weight, qkv_bias, out_weight, out_bias, up_weight, up_bias, down_weight, down_bias, gain_first, shift_first, gain_second, shift_second, cotangent):
    count = tokens.shape[0] // SEQ
    width = tokens.shape[1]
    stacked = tokens.reshape(count, SEQ, width)
    cots = cotangent.reshape(count, SEQ, width)
    params = (qkv_weight, qkv_bias, out_weight, out_bias, up_weight, up_bias, down_weight, down_bias, gain_first, shift_first, gain_second, shift_second)
    start = (jnp.zeros(qkv_weight.shape, jnp.float32), jnp.zeros(qkv_bias.shape, jnp.float32), jnp.zeros(out_weight.shape, jnp.float32), jnp.zeros((width,), jnp.float32), jnp.zeros(up_weight.shape, jnp.float32), jnp.zeros(up_bias.shape, jnp.float32), jnp.zeros(down_weight.shape, jnp.float32), jnp.zeros((width,), jnp.float32), jnp.zeros((width,), jnp.float32), jnp.zeros((width,), jnp.float32), jnp.zeros((width,), jnp.float32))

    def step(carry, item):
        rows, cot = item
        outputs, grad_tokens, grads = sequence(rows, cot, *params)
        return (tuple((left + right for left, right in zip(carry, grads))), (outputs, grad_tokens))
    sums, (outputs, grad_tokens) = lax.scan(step, start, (stacked, cots))
    return (outputs.reshape(tokens.shape), grad_tokens.reshape(tokens.shape), sums[0], sums[1], sums[2], sums[3], sums[4], sums[5], sums[6], sums[3], sums[7], sums[8], sums[9], sums[10])
```

```python
import math

import jax
import jax.numpy as jnp
from jax import lax
from jax.experimental import pallas as pl
from jax.experimental.pallas import tpu as pltpu
from jax.sharding import PartitionSpec as P

HD = 64
ROT = 16

epsilon = 1e-05
ROWS = (((0,), (0,)), ((), ()))
COLS = (((1,), (1,)), ((), ()))
PLAIN = (((1,), (0,)), ((), ()))


def dot(left, right, dims):
    return lax.dot_general(left, right, dims, preferred_element_type=jnp.float32)


def normalize(rows):
    mean = jnp.mean(rows, axis=-1, keepdims=True)
    centred = rows - mean
    variance = jnp.mean(centred * centred, axis=-1, keepdims=True)
    inverse = lax.rsqrt(variance + epsilon)
    return (centred * inverse, inverse)


def gelu_exact(values):
    return jax.nn.gelu(values, approximate=False)


def swap(values, axis, mask):
    size = lax.axis_size(axis)
    return lax.ppermute(values, axis, [(i, i ^ mask) for i in range(size)])


def bits_of(size):
    assert size & (size - 1) == 0
    return [1 << k for k in range(size.bit_length() - 1)]


def order_of(stages):
    order = [0]
    for bit in stages:
        order = order + [item ^ bit for item in order]
    return order


def gather(shard, dim, stages):
    held = shard
    for bit in stages:
        held = jnp.concatenate([held, swap(held, "dp", bit)], dim)
    return held


def scatter(keep, send, dim, stages):
    total = keep + swap(send, "dp", stages[-1]).astype(jnp.float32)
    for bit in stages[-2::-1]:
        half = total.shape[dim] // 2
        send = lax.slice_in_dim(total, half, 2 * half, axis=dim).astype(jnp.bfloat16)
        keep = lax.slice_in_dim(total, 0, half, axis=dim)
        total = keep + swap(send, "dp", bit).astype(jnp.float32)
    return total


def flips(values, me, count):
    lead = values.shape[:-1]
    width = values.shape[-1] // count
    for bit in bits_of(count):
        parts = values.reshape(lead + (count // (2 * bit), 2, bit * width))
        turned = jnp.concatenate([parts[..., 1:, :], parts[..., :1, :]], -2)
        values = jnp.where((me & bit) != 0, turned.reshape(values.shape), values)
    return values


def reorder(values, order):
    width = values.shape[-1] // len(order)
    return jnp.concatenate(
        [values[..., item * width : (item + 1) * width] for item in order], -1
    )


def to_mine(values, me, order):
    return reorder(flips(values, me, len(order)), order)


def from_mine(values, me, order):
    inverse = [order.index(item) for item in range(len(order))]
    return flips(reorder(values, inverse), me, len(order))


def allsum(values, axis):
    bits = bits_of(lax.axis_size(axis))
    while bits:
        group, bits = bits[:3], bits[3:]
        terms = [values] + [
            swap(values, axis, group[0] * item) for item in range(1, 1 << len(group))
        ]
        while len(terms) > 1:
            terms = [terms[i] + terms[i + 1] for i in range(0, len(terms), 2)]
        values = terms[0]
    return values


def attention_kernel(
    projected, dcontext, cosine, sine, row_pos, col_pos, context, dprojected, bias_sums
):
    length, local = dcontext.shape
    scale = 1.0 / math.sqrt(HD)
    lane = lax.broadcasted_iota(jnp.int32, (length, local), 1) % HD
    low = lane < ROT // 2
    cos, sin = cosine[...], sine[...]

    def partner(values):
        return jnp.where(
            low,
            pltpu.roll(values, local - ROT // 2, 1),
            pltpu.roll(values, ROT // 2, 1),
        )

    def turn(values):
        return (values * cos + partner(values) * sin).astype(jnp.bfloat16)

    def turn_back(values):
        return values * cos - partner(values) * sin

    query = turn(projected[0])
    keys = turn(projected[1])
    values = projected[2].astype(jnp.bfloat16)
    grads = dcontext[...]
    mask = row_pos[...] >= col_pos[...]
    contexts, dqs, dks, dvs = [], [], [], []
    for head in range(local // HD):
        cut = slice(head * HD, (head + 1) * HD)
        q = query[:, cut] * jnp.bfloat16(scale)
        k, v, g = keys[:, cut], values[:, cut], grads[:, cut]
        scores = jnp.where(mask, dot(q, k, COLS), -1e30)
        top = jnp.max(scores, -1, keepdims=True)
        powers = jnp.exp(scores - top)
        weights = powers * (1.0 / jnp.sum(powers, -1, keepdims=True))
        probs = weights.astype(jnp.bfloat16)
        contexts.append(dot(probs, v, PLAIN))
        dvs.append(dot(probs, g, ROWS))
        dprobs = dot(g, v, COLS)
        delta = jnp.sum(weights * dprobs, -1, keepdims=True)
        dscores = (weights * (dprobs - delta)).astype(jnp.bfloat16)
        dqs.append(dot(dscores, k, PLAIN) * scale)
        dks.append(dot(dscores, q, ROWS))
    context[...] = jnp.concatenate(contexts, 1).astype(jnp.bfloat16)
    for j, grad in enumerate(
        (
            turn_back(jnp.concatenate(dqs, 1)),
            turn_back(jnp.concatenate(dks, 1)),
            jnp.concatenate(dvs, 1),
        )
    ):
        bias_sums[j] = jnp.sum(grad, 0, keepdims=True)
        dprojected[j] = grad.astype(jnp.bfloat16)


def attention(projected, dcontext, positions):
    length, local = dcontext.shape
    half = ROT // 2
    freqs = 10000.0 ** (-2.0 * jnp.arange(half).astype(jnp.float32) / ROT)
    angles = positions.astype(jnp.float32)[:, None] * freqs[None, :]
    cosine, sine = jnp.cos(angles), jnp.sin(angles)
    rest = jnp.zeros((length, HD - ROT), jnp.float32)
    heads = local // HD
    cosine = jnp.tile(jnp.concatenate([cosine, cosine, rest + 1.0], 1), (1, heads))
    sine = jnp.tile(jnp.concatenate([-sine, sine, rest], 1), (1, heads))
    return pl.pallas_call(
        attention_kernel,
        out_shape=(
            jax.ShapeDtypeStruct((length, local), jnp.bfloat16),
            jax.ShapeDtypeStruct((3, length, local), jnp.bfloat16),
            jax.ShapeDtypeStruct((3, 1, local), jnp.float32),
        ),
        cost_estimate=pl.CostEstimate(
            flops=10 * length * length * local * 4,
            bytes_accessed=16 * length * local,
            transcendentals=length * length * heads,
        ),
        name="attention",
    )(projected, dcontext, cosine, sine, positions[:, None], positions[None, :])


def per_device(
    tokens,
    qkv_weight,
    qkv_bias,
    out_weight,
    out_bias,
    up_weight,
    up_bias,
    down_weight,
    down_bias,
    gain_first,
    shift_first,
    gain_second,
    shift_second,
    cotangent,
):
    rows_here, width = tokens.shape
    shards, ranks = lax.axis_size("dp"), lax.axis_size("tensor")
    me, rank = lax.axis_index("dp"), lax.axis_index("tensor")
    bits = bits_of(shards)
    stages_in = bits[1:] + bits[:1]
    stages_out = bits[:0:-1] + bits[:1]
    order_in, order_out = order_of(stages_in), order_of(stages_out)
    half = width // 2

    def whole(rows):
        return jnp.concatenate([rows] + [swap(rows, "tensor", r) for r in range(1, ranks)], 0)

    qkv_full = gather(qkv_weight, 1, stages_in)
    rows = whole(to_mine(tokens, me, order_in))
    out_full = gather(out_weight, 0, stages_out)
    cot = whole(to_mine(cotangent, me, order_out))
    up_full = gather(up_weight, 0, stages_in)
    down_full = gather(down_weight, 0, stages_out)
    norms = to_mine(
        jnp.stack([gain_first, shift_first, gain_second, shift_second]), me, order_in
    )

    normal, inverse = normalize(rows.astype(jnp.float32))
    first = (normal * norms[0] + norms[1]).astype(jnp.bfloat16)
    second = (normal * norms[2] + norms[3]).astype(jnp.bfloat16)
    local = qkv_full.shape[2]
    projected = jnp.stack([dot(first, qkv_full[j], PLAIN) + qkv_bias[j] for j in range(3)])
    positions = jnp.concatenate(
        [(rank ^ r) * rows_here + jnp.arange(rows_here, dtype=jnp.int32) for r in range(ranks)]
    )
    dcontext = dot(cot, out_full, PLAIN).astype(jnp.bfloat16)
    context, dprojected16, qkvbias_local = attention(projected, dcontext, positions)

    pre = dot(second, up_full, PLAIN) + up_bias
    hidden = gelu_exact(pre).astype(jnp.bfloat16)
    dhidden = dot(cot, down_full, PLAIN)
    _, pullback = jax.vjp(gelu_exact, pre)
    dpre = pullback(dhidden)[0]
    upbias_local = jnp.sum(dpre, 0)
    dpre16 = dpre.astype(jnp.bfloat16)

    def rows_sum(values):
        total = values[:rows_here]
        for r in range(1, ranks):
            part = values[r * rows_here : (r + 1) * rows_here].astype(jnp.bfloat16)
            total = total + swap(part, "tensor", r).astype(jnp.float32)
        return total

    dsecond = dot(dpre16, up_full, COLS)
    dfirst = sum(dot(dprojected16[j], qkv_full[j], COLS) for j in range(3))
    mixed_rows = rows_sum(norms[0] * dfirst + norms[2] * dsecond)
    branch = rows_sum(dot(context, out_full, COLS) + dot(hidden, down_full, COLS))

    def weight_grad(left, right, stages):
        send = dot(left[:, half:], right, ROWS).astype(jnp.bfloat16)
        keep = dot(left[:, :half], right, ROWS)
        return scatter(keep, send, 0, stages)

    grad_down = weight_grad(cot, hidden, stages_out)
    grad_up = weight_grad(second, dpre16, stages_in)
    grad_out = weight_grad(cot, context, stages_out)
    send = jnp.stack(
        [dot(first[:, half:], dprojected16[j], ROWS).astype(jnp.bfloat16) for j in range(3)]
    )
    keep = jnp.stack([dot(first[:, :half], dprojected16[j], ROWS) for j in range(3)])
    grad_qkv = scatter(keep, send, 1, stages_in)

    cot_float = cotangent.astype(jnp.float32)
    norm_terms = jnp.stack(
        [
            jnp.sum(dfirst * normal, 0),
            jnp.sum(dfirst, 0),
            jnp.sum(dsecond * normal, 0),
            jnp.sum(dsecond, 0),
        ]
    )
    norm_terms = jnp.concatenate(
        [from_mine(norm_terms, me, order_in).reshape(-1), jnp.sum(cot_float, 0)]
    )
    sums = jnp.concatenate(
        [allsum(norm_terms, "tensor"), qkvbias_local.reshape(-1), upbias_local]
    )
    sums = allsum(sums, "dp")
    norm_sum = sums[: 4 * width].reshape(4, width)
    bias_sum = sums[4 * width : 5 * width]
    grad_qkvbias = sums[5 * width : 5 * width + 3 * local].reshape(3, local)
    grad_upbias = sums[5 * width + 3 * local :]

    outputs = (
        tokens.astype(jnp.float32) + from_mine(branch, me, order_out) + out_bias + down_bias
    ).astype(jnp.bfloat16)
    normal_rows, inverse_rows = normal[:rows_here], inverse[:rows_here]
    centred = mixed_rows - jnp.mean(mixed_rows, -1, keepdims=True)
    centred = centred - normal_rows * jnp.mean(mixed_rows * normal_rows, -1, keepdims=True)
    grad_tokens = cot_float + from_mine(inverse_rows * centred, me, order_in)
    return (
        outputs,
        grad_tokens,
        grad_qkv,
        grad_qkvbias,
        grad_out,
        bias_sum,
        grad_up,
        grad_upbias,
        grad_down,
        bias_sum,
        norm_sum[0],
        norm_sum[1],
        norm_sum[2],
        norm_sum[3],
    )


def solution(mesh):
    return jax.shard_map(
        per_device,
        mesh=mesh,
        in_specs=(
            P(("dp", "tensor"), None),
            P(None, "dp", "tensor"),
            P(None, "tensor"),
            P("dp", "tensor"),
            P(),
            P("dp", "tensor"),
            P("tensor"),
            P("dp", "tensor"),
            P(),
            P(),
            P(),
            P(),
            P(),
            P(("dp", "tensor"), None),
        ),
        out_specs=(
            P(("dp", "tensor"), None),
            P(("dp", "tensor"), None),
            P(None, "dp", "tensor"),
            P(None, "tensor"),
            P("dp", "tensor"),
            P(),
            P("dp", "tensor"),
            P("tensor"),
            P("dp", "tensor"),
            P(),
            P(),
            P(),
            P(),
            P(),
        ),
        check_vma=False,
    )
```

```python
import math

import jax
import jax.numpy as jnp
from jax import lax
from jax.experimental import pallas as pl
from jax.experimental.pallas import tpu as pltpu
from jax.sharding import PartitionSpec as P

HD = 64
ROT = 16

epsilon = 1e-05
ROWS = (((0,), (0,)), ((), ()))
COLS = (((1,), (1,)), ((), ()))
PLAIN = (((1,), (0,)), ((), ()))


def dot(left, right, dims):
    return lax.dot_general(left, right, dims, preferred_element_type=jnp.float32)


def normalize(rows):
    mean = jnp.mean(rows, axis=-1, keepdims=True)
    centred = rows - mean
    variance = jnp.mean(centred * centred, axis=-1, keepdims=True)
    inverse = lax.rsqrt(variance + epsilon)
    return (centred * inverse, inverse)


def swap(values, axis, mask):
    size = lax.axis_size(axis)
    return lax.ppermute(values, axis, [(i, i ^ mask) for i in range(size)])


def bits_of(size):
    assert size & (size - 1) == 0
    return [1 << k for k in range(size.bit_length() - 1)]


def order_of(stages):
    order = [0]
    for bit in stages:
        order = order + [item ^ bit for item in order]
    return order


def gather(shard, axis, dim, stages):
    held = shard
    for bit in stages:
        held = jnp.concatenate([held, swap(held, axis, bit)], dim)
    return held


def scatter(keep, send, axis, dim, stages):
    total = keep + swap(send, axis, stages[-1]).astype(jnp.float32)
    for bit in stages[-2::-1]:
        half = total.shape[dim] // 2
        send = lax.slice_in_dim(total, half, 2 * half, axis=dim).astype(jnp.bfloat16)
        keep = lax.slice_in_dim(total, 0, half, axis=dim)
        total = keep + swap(send, axis, bit).astype(jnp.float32)
    return total


def flips(values, me, count):
    lead = values.shape[:-1]
    width = values.shape[-1] // count
    for bit in bits_of(count):
        parts = values.reshape(lead + (count // (2 * bit), 2, bit * width))
        turned = jnp.concatenate([parts[..., 1:, :], parts[..., :1, :]], -2)
        values = jnp.where((me & bit) != 0, turned.reshape(values.shape), values)
    return values


def reorder(values, order):
    width = values.shape[-1] // len(order)
    return jnp.concatenate(
        [values[..., item * width : (item + 1) * width] for item in order], -1
    )


def permute(values, me, order, back):
    width = values.shape[-1] // len(order)

    def kernel(index, source, target):
        for i, item in enumerate(order):
            block = pl.ds(pl.multiple_of((index[0] ^ item) * width, width), width)
            mine = slice(i * width, (i + 1) * width)
            if back:
                target[:, block] = source[:, mine]
            else:
                target[:, mine] = source[:, block]

    return pl.pallas_call(
        kernel,
        out_shape=jax.ShapeDtypeStruct(values.shape, values.dtype),
        in_specs=[
            pl.BlockSpec(memory_space=pltpu.SMEM),
            pl.BlockSpec(memory_space=pltpu.VMEM),
        ],
        out_specs=pl.BlockSpec(memory_space=pltpu.VMEM),
        cost_estimate=pl.CostEstimate(
            flops=0, bytes_accessed=2 * values.size * values.dtype.itemsize, transcendentals=0
        ),
        name="permute",
    )(jnp.reshape(me, (1,)).astype(jnp.int32), values)


def to_mine(values, me, order):
    if values.shape[-1] // len(order) % 128 == 0:
        return permute(values, me, order, False)
    return reorder(flips(values, me, len(order)), order)


def from_mine(values, me, order):
    if values.shape[-1] // len(order) % 128 == 0:
        return permute(values, me, order, True)
    inverse = [order.index(item) for item in range(len(order))]
    return flips(reorder(values, inverse), me, len(order))


def allsum(values, axis):
    for bit in bits_of(lax.axis_size(axis)):
        values = values + swap(values, axis, bit)
    return values


def attention_kernel(
    first,
    qkv_weight,
    qkv_bias,
    cot,
    out_weight,
    cosine,
    sine,
    row_pos,
    col_pos,
    context,
    dprojected,
    bias_sums,
):
    length, local = context.shape
    scale = 1.0 / math.sqrt(HD)
    lane = lax.broadcasted_iota(jnp.int32, (length, local), 1) % HD
    low = lane < ROT // 2
    cos, sin = cosine[...], sine[...]

    def partner(values):
        return jnp.where(
            low,
            pltpu.roll(values, local - ROT // 2, 1),
            pltpu.roll(values, ROT // 2, 1),
        )

    def turn(values):
        return (values * cos + partner(values) * sin).astype(jnp.bfloat16)

    def turn_back(values):
        return values * cos - partner(values) * sin

    rows = first[...]
    projected = [dot(rows, qkv_weight[j], PLAIN) + qkv_bias[j : j + 1, :] for j in range(3)]
    query = turn(projected[0])
    keys = turn(projected[1])
    values = projected[2].astype(jnp.bfloat16)
    grads = dot(cot[...], out_weight[...], PLAIN).astype(jnp.bfloat16)
    mask = row_pos[...] >= col_pos[...]
    contexts, dqs, dks, dvs = [], [], [], []
    for head in range(local // HD):
        cut = slice(head * HD, (head + 1) * HD)
        q = query[:, cut] * jnp.bfloat16(scale)
        k, v, g = keys[:, cut], values[:, cut], grads[:, cut]
        scores = jnp.where(mask, dot(q, k, COLS), -1e30)
        top = jnp.max(scores, -1, keepdims=True)
        powers = jnp.exp(scores - top)
        weights = powers * (1.0 / jnp.sum(powers, -1, keepdims=True))
        probs = weights.astype(jnp.bfloat16)
        contexts.append(dot(probs, v, PLAIN))
        dvs.append(dot(probs, g, ROWS))
        dprobs = dot(g, v, COLS)
        delta = jnp.sum(weights * dprobs, -1, keepdims=True)
        dscores = (weights * (dprobs - delta)).astype(jnp.bfloat16)
        dqs.append(dot(dscores, k, PLAIN) * scale)
        dks.append(dot(dscores, q, ROWS))
    context[...] = jnp.concatenate(contexts, 1).astype(jnp.bfloat16)
    for j, grad in enumerate(
        (
            turn_back(jnp.concatenate(dqs, 1)),
            turn_back(jnp.concatenate(dks, 1)),
            jnp.concatenate(dvs, 1),
        )
    ):
        bias_sums[j] = jnp.sum(grad, 0, keepdims=True)
        dprojected[j] = grad.astype(jnp.bfloat16)


def attention(first, qkv_weight, qkv_bias, cot, both_weight, positions):
    length, width = first.shape
    local = qkv_bias.shape[1]
    last = both_weight.shape[1] // local - 1
    half = ROT // 2
    freqs = 10000.0 ** (-2.0 * jnp.arange(half).astype(jnp.float32) / ROT)
    angles = positions.astype(jnp.float32)[:, None] * freqs[None, :]
    cosine, sine = jnp.cos(angles), jnp.sin(angles)
    rest = jnp.zeros((length, HD - ROT), jnp.float32)
    heads = local // HD
    cosine = jnp.tile(jnp.concatenate([cosine, cosine, rest + 1.0], 1), (1, heads))
    sine = jnp.tile(jnp.concatenate([-sine, sine, rest], 1), (1, heads))
    return pl.pallas_call(
        attention_kernel,
        out_shape=(
            jax.ShapeDtypeStruct((length, local), jnp.bfloat16),
            jax.ShapeDtypeStruct((3, length, local), jnp.bfloat16),
            jax.ShapeDtypeStruct((3, 1, local), jnp.float32),
        ),
        grid=(1,),
        in_specs=[
            whole_spec((length, width)),
            whole_spec((3, width, local)),
            whole_spec((3, local)),
            whole_spec((length, width)),
            pl.BlockSpec((width, local), lambda i: (0, last)),
            whole_spec((length, local)),
            whole_spec((length, local)),
            whole_spec((length, 1)),
            whole_spec((1, length)),
        ],
        out_specs=[
            whole_spec((length, local)),
            whole_spec((3, length, local)),
            whole_spec((3, 1, local)),
        ],
        cost_estimate=pl.CostEstimate(
            flops=10 * length * length * local * 4 + 8 * length * width * local,
            bytes_accessed=16 * length * local,
            transcendentals=length * length * heads,
        ),
        name="attention",
    )(
        first,
        qkv_weight,
        qkv_bias,
        cot,
        both_weight,
        cosine,
        sine,
        positions[:, None],
        positions[None, :],
    )


def whole_spec(shape):
    return pl.BlockSpec(shape, lambda i: (0,) * len(shape))


def hidden_kernel(second, up_weight, up_bias, cot, down_weight, context, both, dpre16, sums):
    step = pl.program_id(0)
    last = pl.num_programs(0) - 1

    @pl.when(step < last)
    def _():
        pre = dot(second[...], up_weight[...], PLAIN) + up_bias[...]
        below = 0.5 * (1.0 + lax.erf(pre * math.sqrt(0.5)))
        density = jnp.exp(pre * pre * -0.5) * (1.0 / math.sqrt(2.0 * math.pi))
        both[...] = (pre * below).astype(jnp.bfloat16)
        dpre = dot(cot[...], down_weight[...], PLAIN) * (below + pre * density)
        sums[...] = jnp.sum(dpre, 0, keepdims=True)
        dpre16[...] = dpre.astype(jnp.bfloat16)

    @pl.when(step == last)
    def _():
        both[...] = context[...]


def hidden_part(second, up_weight, up_bias, cot, both_weight, context):
    length, width = second.shape
    units = up_weight.shape[1]
    tile = context.shape[1]
    steps = units // tile

    def column(rows):
        return pl.BlockSpec((rows, tile), lambda i: (0, jnp.minimum(i, steps - 1)))

    return pl.pallas_call(
        hidden_kernel,
        grid=(steps + 1,),
        in_specs=[
            whole_spec((length, width)),
            column(width),
            column(1),
            whole_spec((length, width)),
            column(width),
            whole_spec((length, tile)),
        ],
        out_specs=[
            pl.BlockSpec((length, tile), lambda i: (0, i)),
            column(length),
            column(1),
        ],
        out_shape=(
            jax.ShapeDtypeStruct((length, units + tile), jnp.bfloat16),
            jax.ShapeDtypeStruct((length, units), jnp.bfloat16),
            jax.ShapeDtypeStruct((1, units), jnp.float32),
        ),
        cost_estimate=pl.CostEstimate(
            flops=4 * length * width * units,
            bytes_accessed=4 * (length * width + width * units + length * units),
            transcendentals=2 * length * units,
        ),
        name="hidden",
    )(second, up_weight, up_bias[None, :], cot, both_weight, context)


def back_kernel(dprojected, qkv_weight, dpre16, up_weight, normal, gains, send, keep, terms):
    dfirst = dot(dprojected[0], qkv_weight[0], COLS)
    for j in range(1, 3):
        dfirst = dfirst + dot(dprojected[j], qkv_weight[j], COLS)
    dsecond = dot(dpre16[...], up_weight[...], COLS)
    rows = normal[...]
    terms[0:1, :] = jnp.sum(dfirst * rows, 0, keepdims=True)
    terms[1:2, :] = jnp.sum(dfirst, 0, keepdims=True)
    terms[2:3, :] = jnp.sum(dsecond * rows, 0, keepdims=True)
    terms[3:4, :] = jnp.sum(dsecond, 0, keepdims=True)
    mixed = gains[0:1, :] * dfirst + gains[2:3, :] * dsecond
    half = keep.shape[0]
    keep[...] = mixed[:half]
    send[...] = mixed[half:].astype(jnp.bfloat16)


def back_part(dprojected, qkv_weight, dpre16, up_weight, normal, gains):
    length, width = normal.shape
    local, units = qkv_weight.shape[2], up_weight.shape[1]
    tile = min(width, 256)
    half = length // 2

    def column(rows):
        return pl.BlockSpec((rows, tile), lambda i: (0, i))

    return pl.pallas_call(
        back_kernel,
        grid=(width // tile,),
        in_specs=[
            whole_spec((3, length, local)),
            pl.BlockSpec((3, tile, local), lambda i: (0, i, 0)),
            whole_spec((length, units)),
            pl.BlockSpec((tile, units), lambda i: (i, 0)),
            column(length),
            column(4),
        ],
        out_specs=[column(half), column(half), column(4)],
        out_shape=(
            jax.ShapeDtypeStruct((half, width), jnp.bfloat16),
            jax.ShapeDtypeStruct((half, width), jnp.float32),
            jax.ShapeDtypeStruct((4, width), jnp.float32),
        ),
        cost_estimate=pl.CostEstimate(
            flops=2 * length * width * (units + 3 * local),
            bytes_accessed=10 * length * width + 2 * width * (units + 3 * local),
            transcendentals=0,
        ),
        name="back",
    )(dprojected, qkv_weight, dpre16, up_weight, normal, gains)


def per_device(
    tokens,
    qkv_weight,
    qkv_bias,
    out_weight,
    out_bias,
    up_weight,
    up_bias,
    down_weight,
    down_bias,
    gain_first,
    shift_first,
    gain_second,
    shift_second,
    cotangent,
):
    rows_here, width = tokens.shape
    shards, ranks = lax.axis_size("dp"), lax.axis_size("tensor")
    me, rank = lax.axis_index("dp"), lax.axis_index("tensor")
    bits = bits_of(shards)
    stages_in = bits[1:] + bits[:1]
    stages_out = bits[:0:-1] + bits[:1]
    order_in, order_out = order_of(stages_in), order_of(stages_out)
    half = width // 2

    stages_rows = bits_of(ranks)[::-1]
    order_rows = order_of(stages_rows)

    qkv_full = gather(qkv_weight, "dp", 1, stages_in)
    rows = gather(to_mine(tokens, me, order_in), "tensor", 0, stages_rows)
    both_full = gather(
        jnp.concatenate([down_weight, out_weight], 1), "dp", 0, stages_out
    )
    cot = gather(to_mine(cotangent, me, order_out), "tensor", 0, stages_rows)
    up_full = gather(up_weight, "dp", 0, stages_in)
    norms = to_mine(
        jnp.stack([gain_first, shift_first, gain_second, shift_second]), me, order_in
    )

    normal, inverse = normalize(rows.astype(jnp.float32))
    first = (normal * norms[0] + norms[1]).astype(jnp.bfloat16)
    second = (normal * norms[2] + norms[3]).astype(jnp.bfloat16)
    local = qkv_full.shape[2]
    units = up_full.shape[1]
    positions = jnp.concatenate(
        [(rank ^ r) * rows_here + jnp.arange(rows_here, dtype=jnp.int32) for r in order_rows]
    )
    context, dprojected16, qkvbias_local = attention(
        first, qkv_full, qkv_bias, cot, both_full, positions
    )
    both, dpre16, upbias_local = hidden_part(
        second, up_full, up_bias, cot, both_full, context
    )

    def weight_grad(left, right):
        send = dot(left[:, half:], right, ROWS).astype(jnp.bfloat16)
        keep = dot(left[:, :half], right, ROWS)
        return keep, send

    rows_half = both.shape[0] // 2
    branch = scatter(
        dot(both[:rows_half], both_full, COLS),
        dot(both[rows_half:], both_full, COLS).astype(jnp.bfloat16),
        "tensor",
        0,
        stages_rows,
    )
    grad_both = scatter(*weight_grad(cot, both), "dp", 0, stages_out)
    mixed_send, mixed_keep, norm_terms = back_part(
        dprojected16, qkv_full, dpre16, up_full, normal, norms
    )
    mixed_rows = scatter(mixed_keep, mixed_send, "tensor", 0, stages_rows)
    grad_up = scatter(*weight_grad(second, dpre16), "dp", 0, stages_in)
    parts = [weight_grad(first, dprojected16[j]) for j in range(3)]
    grad_qkv = scatter(
        jnp.stack([part[0] for part in parts]),
        jnp.stack([part[1] for part in parts]),
        "dp",
        1,
        stages_in,
    )
    grad_down, grad_out = grad_both[:, :units], grad_both[:, units:]

    cot_float = cotangent.astype(jnp.float32)
    norm_terms = jnp.concatenate(
        [from_mine(norm_terms, me, order_in).reshape(-1), jnp.sum(cot_float, 0)]
    )
    sums = jnp.concatenate(
        [allsum(norm_terms, "tensor"), qkvbias_local.reshape(-1), upbias_local.reshape(-1)]
    )
    sums = allsum(sums, "dp")
    norm_sum = sums[: 4 * width].reshape(4, width)
    bias_sum = sums[4 * width : 5 * width]
    grad_qkvbias = sums[5 * width : 5 * width + 3 * local].reshape(3, local)
    grad_upbias = sums[5 * width + 3 * local :]

    outputs = (
        tokens.astype(jnp.float32) + from_mine(branch, me, order_out) + out_bias + down_bias
    ).astype(jnp.bfloat16)
    normal_rows, inverse_rows = normal[:rows_here], inverse[:rows_here]
    centred = mixed_rows - jnp.mean(mixed_rows, -1, keepdims=True)
    centred = centred - normal_rows * jnp.mean(mixed_rows * normal_rows, -1, keepdims=True)
    grad_tokens = cot_float + from_mine(inverse_rows * centred, me, order_in)
    return (
        outputs,
        grad_tokens,
        grad_qkv,
        grad_qkvbias,
        grad_out,
        bias_sum,
        grad_up,
        grad_upbias,
        grad_down,
        bias_sum,
        norm_sum[0],
        norm_sum[1],
        norm_sum[2],
        norm_sum[3],
    )


def solution(mesh):
    return jax.shard_map(
        per_device,
        mesh=mesh,
        in_specs=(
            P(("dp", "tensor"), None),
            P(None, "dp", "tensor"),
            P(None, "tensor"),
            P("dp", "tensor"),
            P(),
            P("dp", "tensor"),
            P("tensor"),
            P("dp", "tensor"),
            P(),
            P(),
            P(),
            P(),
            P(),
            P(("dp", "tensor"), None),
        ),
        out_specs=(
            P(("dp", "tensor"), None),
            P(("dp", "tensor"), None),
            P(None, "dp", "tensor"),
            P(None, "tensor"),
            P("dp", "tensor"),
            P(),
            P("dp", "tensor"),
            P("tensor"),
            P("dp", "tensor"),
            P(),
            P(),
            P(),
            P(),
            P(),
        ),
        check_vma=False,
    )
```
